256 devices in a mesh: dp: 8 (over z_lo, x), expert: 32 (over y, z_hi, core).
Axes of the slice: x: 4, y: 4, z: 8 (z_hi: 4, z_lo: 2; z = z_hi * 2 + z_lo), core: 2. Of those that a mesh axis runs over, the one named last changes fastest.
Arguments:
- tokens: bfloat16 [4096, 7168], P('expert', 'dp'), may hold values from -6 to 6
- cotangent: bfloat16 [4096, 7168], P('expert', 'dp'), may hold values from -6 to 6
- routes: int32 [4096, 4], P('expert'), may hold values from 0 to 31, all different within a row; in each aligned block of 128 rows (0 to 127, 128 to 255, ...) at most 24 rows name the same one
- combine_weights: float32 [4096, 4], P('expert'), may hold values from 0.2 to 1
- gate_weight: bfloat16 [32, 7168, 1024], P('expert', 'dp'), may hold values from -0.0625 to 0.0625
- up_weight: bfloat16 [32, 7168, 1024], P('expert', 'dp'), may hold values from -0.0625 to 0.0625
- down_weight: bfloat16 [32, 1024, 7168], P('expert', None, 'dp'), may hold values from -0.1875 to 0.1875
Outputs:
- grad_tokens: bfloat16 [4096, 7168], P('expert', 'dp')
- grad_gate: bfloat16 [32, 7168, 1024], P('expert', 'dp')
- grad_up: bfloat16 [32, 7168, 1024], P('expert', 'dp')
- grad_down: bfloat16 [32, 1024, 7168], P('expert', None, 'dp')
The draws below stay inside these ranges and needn't reach their ends.
Inputs may be any that keep to these rules, and one draw needn't show every extreme that they name: `routes`: each row names 4 different experts. Within each aligned block of 128 tokens no expert is named by more than 24 tokens, and in every draw some block has an expert named by exactly 24 tokens.
All inputs are finite; a program needn't handle non-finite values.
Results may differ from the reference program's by a relative error of at most 0.029.
Values may be sent and summed in bfloat16 or wider, within the bound.
No kernel may reach another device: no remote copies, remote signals or barrier semaphores. Data moves between devices by JAX's collectives and lax.ppermute only.
A program may use at most 64 MiB of HBM per device.

```python
import math
import jax
import jax.numpy as jnp
import numpy as np
from jax import lax

D = 7168
HID = 1024
TOP = 4
TOK_DEV = 128
EXPERTS = 32
CAP = 24
TOKENS = 4096
N_DP = 8
N_EXPERT = 32


def shard_levels(rng, dims, split, low, high):
    factor_of = 1.0
    for position, shards_of in split:
        draws = jax.random.uniform(jax.random.fold_in(jax.random.fold_in(rng, 6), position), (shards_of,), jnp.float32, low / len(split), high / len(split))
        factor_of = factor_of * jnp.repeat(jnp.exp(draws), dims[position] // shards_of).reshape((-1,) + (1,) * (len(dims) - 1 - position))
    return factor_of


def assign_block(rng, own, number, rows, amount, top, most, skew):
    ranking = jax.random.permutation(rng, amount)
    crowded, usual = portions_of(amount, rows * top, most, skew, True), portions_of(amount, rows * top, most, skew, False)
    places = jnp.arange(amount)

    def named(tallies, offset_by):
        used = int((tallies > 0).sum())
        fixed = max(1, used // 4)
        moved = fixed + (places - fixed + offset_by * (used - fixed)) % max(1, amount - fixed)
        return jnp.zeros((amount,), jnp.int32).at[ranking[jnp.where(places < fixed, places, moved)]].set(jnp.asarray(tallies, jnp.int32))

    tallies = jnp.where(number % 4 == 0, named(crowded, number // 4), named(usual, number - number // 4 - 1))
    mixed = jax.random.permutation(jax.random.fold_in(own, 3), amount)
    donor, sink = mixed[0:amount // 2 * 2:2], mixed[1:amount // 2 * 2:2]
    slack = jnp.minimum(tallies[donor] - 1, most - tallies[sink]) // 2
    slack = jnp.where((donor == ranking[0]) | (sink == ranking[0]) | (tallies[sink] == 0), 0, jnp.maximum(slack, 0))
    moved = jax.random.randint(jax.random.fold_in(own, 4), (amount // 2,), 0, 1 << 20) % (slack + 1)
    tallies = tallies.at[donor].add(-moved).at[sink].add(moved)
    labels = jnp.searchsorted(jnp.cumsum(tallies), jnp.arange(rows * top), side="right").astype(jnp.int32)
    grid = labels.reshape(top, rows).T
    grid = grid[jax.random.permutation(jax.random.fold_in(own, 1), rows)]
    offset_by = jax.random.randint(jax.random.fold_in(own, 2), (rows, 1), 0, top)
    return jnp.take_along_axis(grid, (jnp.arange(top)[None, :] + offset_by) % top, axis=1)


def portions_of(amount, total, reach, lean, full):
    loads = [(1 << 20) // math.isqrt(rank ** lean) + 1 for rank in range(1, amount + 1)]
    largest = reach if full else min(reach, max(-(-total // amount), total * loads[0] // sum(loads)))
    least = 1 if total - largest >= amount - 1 else 0
    holding, spare = [largest] + [least] * (amount - 1), total - largest - least * (amount - 1)
    while spare > 0:
        movable = [i for i in range(1, amount) if holding[i] < largest] or [i for i in range(1, amount) if holding[i] < reach]
        mass, left = sum([loads[i] for i in movable]), spare
        for i in movable:
            extra = min(reach - holding[i], max(1, left * loads[i] // mass), spare)
            holding[i] = holding[i] + extra
            spare = spare - extra
    return np.array(holding)


def scatter_about(own_key, shape, spread, bound, pieces=(), kind=jnp.bfloat16):
    gain = shard_levels(own_key, shape, pieces, -0.22, 0.18) if pieces else 1.0
    entries = jax.random.normal(own_key, shape, jnp.float32) * spread * gain
    return jnp.minimum(jnp.maximum(entries, -bound), bound).astype(kind)


def setup_inputs(seed: int = 0) -> dict:
    arg_keys = jax.random.split(jax.random.key(seed), 8)
    tokens = scatter_about(arg_keys[0], (TOKENS, D), 1.0, 6.0, ((0, 32), (1, 8)))
    cotangent = scatter_about(arg_keys[1], (TOKENS, D), 1.0, 6.0, ((0, 32), (1, 8)))
    routes_keys = jax.random.split(jax.random.fold_in(arg_keys[2], 1), TOKENS // TOK_DEV)
    routes_turns = jax.random.permutation(jax.random.fold_in(arg_keys[2], 3), TOKENS // TOK_DEV)
    routes = jax.vmap(lambda own, number: assign_block(jax.random.fold_in(arg_keys[2], 2), own, number, TOK_DEV, EXPERTS, TOP, CAP, 2))(routes_keys, routes_turns).reshape((TOKENS, TOP))
    combine_weights = jnp.clip(0.2 + 0.8 * jax.random.uniform(arg_keys[3], (TOKENS, TOP), jnp.float32) ** shard_levels(arg_keys[3], (TOKENS, TOP), ((0, 32),), -0.2, 0.2), 0.2, 1.0)
    gate_weight = scatter_about(arg_keys[4], (EXPERTS, D, HID), D ** -0.5, 0.0625, ((0, 32), (1, 8)))
    up_weight = scatter_about(arg_keys[5], (EXPERTS, D, HID), D ** -0.5, 0.0625, ((0, 32), (1, 8)))
    down_weight = scatter_about(arg_keys[6], (EXPERTS, HID, D), HID ** -0.5, 0.1875, ((0, 32), (2, 8)))
    return {"tokens": tokens, "cotangent": cotangent, "routes": routes, "combine_weights": combine_weights, "gate_weight": gate_weight, "up_weight": up_weight, "down_weight": down_weight}


def block_sum(left_blocks, right_blocks, form):
    terms = jnp.einsum(form, left_blocks, right_blocks)
    rounded = lax.optimization_barrier(terms.astype(jnp.bfloat16))
    return jnp.sum(rounded.astype(jnp.float32), axis=1)


def expert_backward(x_rows, s_rows, weight_g, weight_u, weight_d):
    count = x_rows.shape[0]
    width = D // N_DP
    x_blocks = x_rows.reshape(count, N_DP, width).astype(jnp.float32)
    s_blocks = s_rows.reshape(count, N_DP, width).astype(jnp.float32)
    gate = block_sum(x_blocks, weight_g.reshape(N_DP, width, HID).astype(jnp.float32), "mbd,bdh->mbh")
    upper = block_sum(x_blocks, weight_u.reshape(N_DP, width, HID).astype(jnp.float32), "mbd,bdh->mbh")
    activation = jax.nn.silu(gate)
    hidden = (activation * upper).astype(jnp.bfloat16)
    dhidden = block_sum(s_blocks, weight_d.reshape(HID, N_DP, width).astype(jnp.float32), "mbd,hbd->mbh")
    sigmoid_g = jax.nn.sigmoid(gate)
    slope = sigmoid_g * (1.0 + gate * (1.0 - sigmoid_g))
    pre_gate = (dhidden * upper * slope).astype(jnp.bfloat16)
    pre_up = (dhidden * activation).astype(jnp.bfloat16)
    grad_down = jnp.dot(hidden.T, s_rows, preferred_element_type=jnp.float32).astype(jnp.bfloat16)
    grad_gate = jnp.dot(x_rows.T, pre_gate, preferred_element_type=jnp.float32).astype(jnp.bfloat16)
    grad_up = jnp.dot(x_rows.T, pre_up, preferred_element_type=jnp.float32).astype(jnp.bfloat16)
    back_rows = jnp.dot(pre_gate, weight_g.T, preferred_element_type=jnp.float32)
    back_rows = (back_rows + jnp.dot(pre_up, weight_u.T, preferred_element_type=jnp.float32)).astype(jnp.bfloat16)
    return grad_gate, grad_up, grad_down, back_rows


def fill_slots(slot_row, values):
    return jnp.zeros((EXPERTS * CAP, D), jnp.bfloat16).at[slot_row].set(values)


def pick_slots(buffer, slot_row):
    return buffer[slot_row]


def reference(tokens, cotangent, routes, combine_weights, gate_weight, up_weight, down_weight):
    pairs = TOK_DEV * TOP
    flat = routes.reshape(N_EXPERT, pairs).astype(jnp.int32)
    onehot = (flat[:, :, None] == jnp.arange(EXPERTS, dtype=jnp.int32)[None, None, :]).astype(jnp.int32)
    before = jnp.cumsum(onehot, axis=1) - onehot
    slot_rank = jnp.sum(before * onehot, axis=2)
    slots = (flat * CAP + slot_rank).astype(jnp.int32)
    scaled = (combine_weights[:, :, None] * cotangent[:, None, :].astype(jnp.float32)).astype(jnp.bfloat16)
    x_pairs = jnp.broadcast_to(tokens[:, None, :], (TOKENS, TOP, D)).reshape(N_EXPERT, pairs, D)
    s_pairs = scaled.reshape(N_EXPERT, pairs, D)
    send_x = jax.vmap(fill_slots)(slots, x_pairs)
    send_s = jax.vmap(fill_slots)(slots, s_pairs)
    by_x = send_x.reshape(N_EXPERT, EXPERTS, CAP, D).transpose(1, 0, 2, 3).reshape(EXPERTS, N_EXPERT * CAP, D)
    by_s = send_s.reshape(N_EXPERT, EXPERTS, CAP, D).transpose(1, 0, 2, 3).reshape(EXPERTS, N_EXPERT * CAP, D)

    def one_expert(packed):
        return expert_backward(packed[0], packed[1], packed[2], packed[3], packed[4])

    grad_gate, grad_up, grad_down, back_rows = lax.map(one_expert, (by_x, by_s, gate_weight, up_weight, down_weight))
    back = back_rows.reshape(EXPERTS, N_EXPERT, CAP, D).transpose(1, 0, 2, 3).reshape(N_EXPERT, EXPERTS * CAP, D)
    picked = jax.vmap(pick_slots)(back, slots)
    grad_tokens = jnp.sum(picked.reshape(TOKENS, TOP, D).astype(jnp.float32), axis=1).astype(jnp.bfloat16)
    return grad_tokens, grad_gate, grad_up, grad_down
```

```python
import functools

import jax
import jax.numpy as jnp
from jax import lax
from jax.experimental import pallas as pl
from jax.experimental.pallas import tpu as pltpu
from jax.sharding import PartitionSpec as P

bf16 = jnp.bfloat16
f32 = jnp.float32
NX = 4
NZ = 2
BLK = 256


def call(body, ins, outs, scratch=(), steps=1, n_smem=0):
    def whole(shape):
        return pl.BlockSpec(shape, lambda i, n=len(shape): (0,) * n)

    def rowwise(shape, axis):
        block = tuple(v // steps if k == axis else v for k, v in enumerate(shape))
        return pl.BlockSpec(block, lambda i, n=len(shape), axis=axis: tuple(i if k == axis else 0 for k in range(n)))

    def run(*args):
        specs = [pl.BlockSpec(memory_space=pltpu.SMEM)] * n_smem
        for v, axis in zip(args[n_smem:], ins, strict=True):
            specs.append(whole(v.shape) if axis is None else rowwise(v.shape, axis))
        return pl.pallas_call(
            body,
            grid=(steps,),
            out_shape=tuple(jax.ShapeDtypeStruct(s, d) for s, d, _ in outs),
            in_specs=specs,
            out_specs=tuple(whole(s) if axis is None else rowwise(s, axis) for s, _, axis in outs),
            scratch_shapes=list(scratch),
            compiler_params=pltpu.CompilerParams(vmem_limit_bytes=24 * 1024 * 1024),
        )(*args)

    return run


def dot(a, b, ca, cb):
    return lax.dot_general(a, b, (((ca,), (cb,)), ((), ())), preferred_element_type=f32)


def prep_body(routes_ref, weights_ref, tokens_ref, x_ref, sel_ref, w_ref, *, experts, cap):
    top, tok = routes_ref.shape
    e_id = lax.broadcasted_iota(jnp.int32, (experts, tok), 0)
    names = jnp.zeros((experts, tok), f32)
    scale = jnp.zeros((experts, tok), f32)
    for k in range(top):
        hit = routes_ref[k : k + 1, :] == e_id
        names = jnp.where(hit, 1.0, names)
        scale = jnp.where(hit, weights_ref[k : k + 1, :], scale)
    row = lax.broadcasted_iota(jnp.int32, (tok, tok), 0)
    col = lax.broadcasted_iota(jnp.int32, (tok, tok), 1)
    earlier = jnp.where(row < col, 1.0, 0.0).astype(bf16)
    rank = dot(names.astype(bf16), earlier, 1, 0)
    rank = jnp.where(names > 0.0, rank, -1.0)
    slot = lax.broadcasted_iota(jnp.int32, (cap, tok), 0).astype(f32)
    for e in range(experts):
        here = rank[e : e + 1, :] == slot
        sel_ref[e * cap : (e + 1) * cap, :] = jnp.where(here, 1.0, 0.0)
        w_ref[e * cap : (e + 1) * cap, :] = jnp.sum(
            jnp.where(here, scale[e : e + 1, :], 0.0), axis=1, keepdims=True
        )
    x_ref[...] = dot(sel_ref[...].astype(bf16), tokens_ref[...], 1, 0).astype(bf16)


def scale_body(sel_ref, w_ref, cot_ref, s_ref):
    s_ref[...] = (dot(sel_ref[...].astype(bf16), cot_ref[...], 1, 0) * w_ref[...]).astype(bf16)


def lanes(tab, j):
    return pl.ds(pl.multiple_of(tab[j] * 128, 128), 128)


def gate_up_body(tab, x_ref, wg_ref, wu_ref, *refs):
    outs, (g_s, u_s) = refs[:-2], refs[-2:]
    g_s[...] = dot(x_ref[...], wg_ref[...], 1, 0).astype(bf16)
    u_s[...] = dot(x_ref[...], wu_ref[...], 1, 0).astype(bf16)
    for t in range(NZ):
        for s, o in enumerate(outs):
            o[t, :, 0:128] = g_s[:, lanes(tab, t * NX + s)]
            o[t, :, 128:256] = u_s[:, lanes(tab, t * NX + s)]


def dhid_body(tab, s_ref, wd_ref, *refs):
    outs, d_s = refs[:-1], refs[-1]
    d_s[...] = dot(s_ref[...], wd_ref[...], 1, 1).astype(bf16)
    for t in range(NZ):
        for s, o in enumerate(outs):
            o[t] = d_s[:, lanes(tab, t * NX + s)]


def back_body(tab, *refs):
    pieces, (wg_ref, wu_ref, back_ref, pg_ref, pu_ref) = refs[:-5], refs[-5:]
    for z in range(NZ):
        own, left, right, far_g, far_u = pieces[5 * z : 5 * z + 5]
        for q, v in enumerate((own, left, right)):
            pg_ref[:, lanes(tab, 4 * z + q)] = v[0]
            pu_ref[:, lanes(tab, 4 * z + q)] = v[1]
        pg_ref[:, lanes(tab, 4 * z + 3)] = far_g[...]
        pu_ref[:, lanes(tab, 4 * z + 3)] = far_u[...]
    t = dot(pg_ref[...], wg_ref[...], 1, 1) + dot(pu_ref[...], wu_ref[...], 1, 1)
    back_ref[...] = t.astype(bf16)


def hid_body(tab, *refs):
    pieces, o_ref = refs[:-1], refs[-1]
    half = o_ref.shape[0] // 2
    for z in range(NZ):
        own, left, right, far_a, far_b = pieces[5 * z : 5 * z + 5]
        for q, p in enumerate((own, left, right)):
            o_ref[:, lanes(tab, 4 * z + q)] = p[...]
        o_ref[0:half, lanes(tab, 4 * z + 3)] = far_a[...]
        o_ref[half : 2 * half, lanes(tab, 4 * z + 3)] = far_b[...]


def combine_body(sel_ref, ret_ref, o_ref):
    o_ref[...] = dot(sel_ref[...].astype(bf16), ret_ref[...], 0, 0).astype(bf16)


def dp_perm(dz, dx):
    return [
        (z * NX + x, ((z + dz) % NZ) * NX + (x + dx) % NX) for z in range(NZ) for x in range(NX)
    ]


def move(v, dz, dx):
    return lax.ppermute(v, "dp", dp_perm(dz, dx))


def scatter_sum(parts):
    parts = [parts[0]] + [move(parts[s], 0, s) for s in range(1, NX)]

    def total(t):
        return sum(p[t].astype(f32) for p in parts)

    return total(0) + move(total(1).astype(bf16), 1, 0).astype(f32)


def local(tokens, cotangent, routes, combine_weights, gate_weight, up_weight, down_weight):
    experts = lax.axis_size("expert")
    tok, top = routes.shape
    width = tokens.shape[1]
    hid = gate_weight.shape[2]
    cap = 3 * tok * top // (2 * experts)
    rows = experts * cap
    steps = rows // BLK
    wg, wu, wd = gate_weight[0], up_weight[0], down_weight[0]
    d = lax.axis_index("dp")
    z, x = d // NX, d % NX

    def table(shifts):
        s = jnp.array(shifts, jnp.int32)
        return (((z + jnp.arange(NZ))[:, None] % NZ) * NX + (x + s)[None, :] % NX).reshape(-1)

    dest = table((0, 1, 2, 3))
    orig = table((0, NX - 1, 1, 2))

    send_x, sel, w_slot = call(
        functools.partial(prep_body, experts=experts, cap=cap),
        [None] * 3,
        [((rows, width), bf16, None), ((rows, tok), f32, None), ((rows, 1), f32, None)],
    )(routes.T, combine_weights.T, tokens)
    (send_s,) = call(scale_body, [0, 0, None], [((rows, width), bf16, 0)], steps=steps)(
        sel, w_slot, cotangent
    )

    def a2a(v):
        return lax.all_to_all(
            v.reshape(experts, cap, width), "expert", split_axis=0, concat_axis=0, tiled=True
        ).reshape(rows, width)

    rows_x = a2a(send_x)
    gu = call(
        gate_up_body,
        [0, None, None],
        [((NZ, rows, 256), bf16, 1)] * NX,
        scratch=[pltpu.VMEM((BLK, hid), bf16)] * 2,
        steps=steps,
        n_smem=1,
    )(dest, rows_x, wg, wu)
    rows_s = a2a(send_s)
    dh = call(
        dhid_body,
        [0, None],
        [((NZ, rows, 128), bf16, 1)] * NX,
        scratch=[pltpu.VMEM((BLK, hid), bf16)],
        steps=steps,
        n_smem=1,
    )(dest, rows_s, wd)
    gu = scatter_sum(gu)
    gate, upper = gu[:, :128], gu[:, 128:]
    sig = jax.nn.sigmoid(gate)
    act = gate * sig
    hidden = (act * upper).astype(bf16)
    slope = upper * (sig * (1.0 + gate * (1.0 - sig)))
    dh = scatter_sum(dh)
    pre = jnp.stack([(dh * slope).astype(bf16), (dh * act).astype(bf16)])

    pieces = []
    for v in (pre, move(pre, 1, 0)):
        left, right = move(v, 0, 1), move(v, 0, NX - 1)
        pieces += [v, left, right, move(left[0], 0, 1), move(right[1], 0, NX - 1)]
    back, pre_gate, pre_up = call(
        back_body,
        [1, 1, 1, 0, 0] * NZ + [None, None],
        [((rows, width), bf16, 0), ((rows, hid), bf16, 0), ((rows, hid), bf16, 0)],
        steps=steps,
        n_smem=1,
    )(orig, *pieces, wg, wu)
    hidden_z = move(hidden, 1, 0)
    back, hidden, hidden_z = lax.optimization_barrier((back, hidden, hidden_z))
    returned = a2a(back)
    half = rows // 2
    pieces = []
    for v in (hidden, hidden_z):
        left, right = move(v, 0, 1), move(v, 0, NX - 1)
        pieces += [v, left, right, move(left[:half], 0, 1), move(right[half:], 0, NX - 1)]
    (hidden_all,) = call(hid_body, [None] * 10, [((rows, hid), bf16, None)], n_smem=1)(orig, *pieces)
    grad_gate = dot(rows_x, pre_gate, 0, 0).astype(bf16)[None]
    grad_up = dot(rows_x, pre_up, 0, 0).astype(bf16)[None]
    grad_down = dot(hidden_all, rows_s, 0, 0).astype(bf16)[None]
    (grad_tokens,) = call(combine_body, [None, None], [((tok, width), bf16, None)])(sel, returned)
    return (grad_tokens, grad_gate, grad_up, grad_down)


def solution(mesh):
    placed = (
        P("expert", "dp"),
        P("expert", "dp"),
        P("expert", None),
        P("expert", None),
        P("expert", "dp", None),
        P("expert", "dp", None),
        P("expert", None, "dp"),
    )
    return jax.shard_map(
        local,
        mesh=mesh,
        in_specs=placed,
        out_specs=(
            P("expert", "dp"),
            P("expert", "dp", None),
            P("expert", "dp", None),
            P("expert", None, "dp"),
        ),
        check_vma=False,
    )
```

```python
import functools

import jax
import jax.numpy as jnp
from jax import lax
from jax.experimental import pallas as pl
from jax.experimental.pallas import tpu as pltpu
from jax.sharding import PartitionSpec as P

bf16 = jnp.bfloat16
f32 = jnp.float32
NX = 4
NZ = 2
BLK = 256


FIRST, LAST = "first", "last"


def call(body, ins, outs, scratch=(), steps=1, n_smem=0, hbm=()):
    def whole(shape):
        return pl.BlockSpec(shape, lambda i, n=len(shape): (0,) * n)

    def rowwise(shape, axis):
        block = tuple(v // steps if k == axis else v for k, v in enumerate(shape))
        return pl.BlockSpec(block, lambda i, n=len(shape), axis=axis: tuple(i if k == axis else 0 for k in range(n)))

    def out_spec(shape, axis):
        if axis in (FIRST, LAST):
            block = (shape[0], shape[1] // 2, shape[2])
            first = axis == FIRST
            return pl.BlockSpec(
                block, lambda i: (0, jnp.minimum(i, 1) if first else jnp.maximum(i - 2, 0), 0)
            )
        return whole(shape) if axis is None else rowwise(shape, axis)

    def run(*args):
        specs = [pl.BlockSpec(memory_space=pltpu.SMEM)] * n_smem
        args = list(args)
        for k in hbm:
            args[n_smem + k] = pltpu.with_memory_space_constraint(args[n_smem + k], pltpu.HBM)
        for v, axis in zip(args[n_smem:], ins, strict=True):
            specs.append(whole(v.shape) if axis is None else rowwise(v.shape, axis))
        return pl.pallas_call(
            body,
            grid=(steps,),
            out_shape=tuple((pltpu.HBM if hbm else jax.ShapeDtypeStruct)(s, d) for s, d, _ in outs),
            in_specs=specs,
            out_specs=tuple(out_spec(s, axis) for s, _, axis in outs),
            scratch_shapes=list(scratch),
            compiler_params=pltpu.CompilerParams(vmem_limit_bytes=24 * 1024 * 1024),
        )(*args)

    return run


def dot(a, b, ca, cb):
    return lax.dot_general(a, b, (((ca,), (cb,)), ((), ())), preferred_element_type=f32)


def prep_body(routes_ref, weights_ref, tokens_ref, x_ref, sel_ref, w_ref, *, experts, cap):
    top, tok = routes_ref.shape
    e_id = lax.broadcasted_iota(jnp.int32, (experts, tok), 0)
    names = jnp.zeros((experts, tok), f32)
    scale = jnp.zeros((experts, tok), f32)
    for k in range(top):
        hit = routes_ref[k : k + 1, :] == e_id
        names = jnp.where(hit, 1.0, names)
        scale = jnp.where(hit, weights_ref[k : k + 1, :], scale)
    row = lax.broadcasted_iota(jnp.int32, (tok, tok), 0)
    col = lax.broadcasted_iota(jnp.int32, (tok, tok), 1)
    earlier = jnp.where(row < col, 1.0, 0.0).astype(bf16)
    rank = dot(names.astype(bf16), earlier, 1, 0)
    rank = jnp.where(names > 0.0, rank, -1.0)
    slot = lax.broadcasted_iota(jnp.int32, (cap, tok), 0).astype(f32)
    for e in range(experts):
        here = rank[e : e + 1, :] == slot
        sel_ref[e * cap : (e + 1) * cap, :] = jnp.where(here, 1.0, 0.0)
        w_ref[e * cap : (e + 1) * cap, :] = jnp.sum(
            jnp.where(here, scale[e : e + 1, :], 0.0), axis=1, keepdims=True
        )
    x_ref[...] = dot(sel_ref[...].astype(bf16), tokens_ref[...], 1, 0).astype(bf16)


def scale_body(sel_ref, w_ref, cot_ref, s_ref):
    s_ref[...] = (dot(sel_ref[...].astype(bf16), cot_ref[...], 1, 0) * w_ref[...]).astype(bf16)


def lanes(tab, j):
    return pl.ds(pl.multiple_of(tab[j] * 128, 128), 128)


def gate_up_body(tab, x_ref, wg_ref, wu_ref, *refs):
    outs, (g_s, u_s) = refs[:NX], refs[NX:]
    g_s[...] = dot(x_ref[...], wg_ref[...], 1, 0).astype(bf16)
    u_s[...] = dot(x_ref[...], wu_ref[...], 1, 0).astype(bf16)
    for t in range(NZ):
        for s, o in enumerate(outs):
            o[t, :, 0:128] = g_s[:, lanes(tab, t * NX + s)]
            o[t, :, 128:256] = u_s[:, lanes(tab, t * NX + s)]


def dhid_body(tab, s_ref, wd_ref, *refs):
    outs, d_s = refs[:NX], refs[NX]
    d_s[...] = dot(s_ref[...], wd_ref[...], 1, 1).astype(bf16)
    for t in range(NZ):
        for s, o in enumerate(outs):
            o[t] = d_s[:, lanes(tab, t * NX + s)]


def back_body(tab, *refs):
    gates, ups = refs[: NZ * NX], refs[NZ * NX : 2 * NZ * NX]
    wg_ref, wu_ref, back_ref, pg_ref, pu_ref = refs[-5:]
    for q in range(NZ * NX):
        pg_ref[:, lanes(tab, q)] = gates[q][...]
        pu_ref[:, lanes(tab, q)] = ups[q][...]
    t = dot(pg_ref[...], wg_ref[...], 1, 1) + dot(pu_ref[...], wu_ref[...], 1, 1)
    back_ref[...] = t.astype(bf16)


def hid_body(tab, *refs):
    pieces, o_ref = refs[:-1], refs[-1]
    half = o_ref.shape[0] // 2
    for z in range(NZ):
        own, left, right, far_a, far_b = pieces[5 * z : 5 * z + 5]
        for q, p in enumerate((own, left, right)):
            o_ref[:, lanes(tab, 4 * z + q)] = p[...]
        o_ref[0:half, lanes(tab, 4 * z + 3)] = far_a[...]
        o_ref[half : 2 * half, lanes(tab, 4 * z + 3)] = far_b[...]


def combine_body(sel_ref, ret_ref, o_ref):
    o_ref[...] = dot(sel_ref[...].astype(bf16), ret_ref[...], 0, 0).astype(bf16)


def dp_perm(dz, dx):
    return [
        (z * NX + x, ((z + dz) % NZ) * NX + (x + dx) % NX) for z in range(NZ) for x in range(NX)
    ]


def move(v, dz, dx):
    return lax.ppermute(v, "dp", dp_perm(dz, dx))


def add(*parts):
    return sum(p.astype(f32) for p in parts)


def sum_x_first(by_s):
    parts = [by_s[0]] + [move(by_s[s], 0, s) for s in range(1, NX)]
    other = move(add(*(p[1] for p in parts)).astype(bf16), 1, 0)
    return add(other, *(p[0] for p in parts))


def sum_z_first(by_t):
    other = move(by_t[1], 1, 0)
    sums = [add(by_t[0][s], other[s]) for s in range(NX)]
    return add(sums[0], *(move(sums[s].astype(bf16), 0, s) for s in range(1, NX)))


def gather(gate, up):
    gl, gr = move(gate, 0, 1), move(gate, 0, NX - 1)
    uz = move(up, 1, 0)
    ul, ur = move(up, 0, 1), move(up, 0, NX - 1)
    gates = [gate, gl, gr, move(gl, 0, 1)]
    gates += [move(v, 1, 0) for v in gates]
    uzl, uzr = move(uz, 0, 1), move(uz, 0, NX - 1)
    ups = [up, ul, ur, move(ur, 0, NX - 1), uz, uzl, uzr, move(uzl, 0, 1)]
    return gates + ups


def local(tokens, cotangent, routes, combine_weights, gate_weight, up_weight, down_weight):
    experts = lax.axis_size("expert")
    tok, top = routes.shape
    width = tokens.shape[1]
    hid = gate_weight.shape[2]
    cap = 3 * tok * top // (2 * experts)
    rows = experts * cap
    steps = rows // BLK
    wg, wu, wd = gate_weight[0], up_weight[0], down_weight[0]
    d = lax.axis_index("dp")
    z, x = d // NX, d % NX

    def table(shifts):
        s = jnp.array(shifts, jnp.int32)
        return (((z + jnp.arange(NZ))[:, None] % NZ) * NX + (x + s)[None, :] % NX).reshape(-1)

    dest = table((0, 1, 2, 3))
    orig = table((0, NX - 1, 1, 2))

    send_x, sel, w_slot = call(
        functools.partial(prep_body, experts=experts, cap=cap),
        [None] * 3,
        [((rows, width), bf16, None), ((rows, tok), f32, None), ((rows, 1), f32, None)],
    )(routes.T, combine_weights.T, tokens)
    (send_s,) = call(scale_body, [0, 0, None], [((rows, width), bf16, 0)], steps=steps)(
        sel, w_slot, cotangent
    )

    def a2a(v):
        return lax.all_to_all(
            v.reshape(experts, cap, width), "expert", split_axis=0, concat_axis=0, tiled=True
        ).reshape(rows, width)

    rows_x = a2a(send_x)
    rows_x, send_s = lax.optimization_barrier((rows_x, send_s))
    gu = call(
        gate_up_body,
        [0, None, None],
        [((NZ, rows, 256), bf16, 1)] * NX,
        scratch=[pltpu.VMEM((BLK, hid), bf16)] * 2,
        steps=steps,
        hbm=(0,),
        n_smem=1,
    )(dest, rows_x, wg, wu)
    rows_s = a2a(send_s)
    half = rows // 2
    dh = call(
        dhid_body,
        [0, None],
        [((NZ, rows, 128), bf16, 1)] * NX,
        scratch=[pltpu.VMEM((BLK, hid), bf16)],
        steps=steps,
        hbm=(0,),
        n_smem=1,
    )(dest, rows_s, wd)
    gu = sum_x_first(gu)
    gate, upper = gu[:, :128], gu[:, 128:]
    sig = jax.nn.sigmoid(gate)
    act = gate * sig
    hidden = (act * upper).astype(bf16)
    slope = upper * (sig * (1.0 + gate * (1.0 - sig)))
    dh = sum_x_first(dh)
    back, pre_gate, pre_up = call(
        back_body,
        [0] * (2 * NZ * NX) + [None, None],
        [((rows, width), bf16, 0), ((rows, hid), bf16, 0), ((rows, hid), bf16, 0)],
        steps=steps,
        hbm=tuple(range(2 * NZ * NX)),
        n_smem=1,
    )(orig, *gather((dh * slope).astype(bf16), (dh * act).astype(bf16)), wg, wu)
    hidden_z = move(hidden, 1, 0)
    back, hidden, hidden_z = lax.optimization_barrier((back, hidden, hidden_z))
    returned = a2a(back)
    pieces = []
    for v in (hidden, hidden_z):
        left, right = move(v, 0, 1), move(v, 0, NX - 1)
        pieces += [v, left, right, move(left[:half], 0, 1), move(right[half:], 0, NX - 1)]
    (hidden_all,) = call(hid_body, [None] * 10, [((rows, hid), bf16, None)], n_smem=1, hbm=tuple(range(10)))(orig, *pieces)
    grad_gate = dot(rows_x, pre_gate, 0, 0).astype(bf16)[None]
    grad_up = dot(rows_x, pre_up, 0, 0).astype(bf16)[None]
    grad_down = dot(hidden_all, rows_s, 0, 0).astype(bf16)[None]
    (grad_tokens,) = call(combine_body, [None, None], [((tok, width), bf16, None)], hbm=(0, 1))(sel, returned)
    return (grad_tokens, grad_gate, grad_up, grad_down)


def solution(mesh):
    placed = (
        P("expert", "dp"),
        P("expert", "dp"),
        P("expert", None),
        P("expert", None),
        P("expert", "dp", None),
        P("expert", "dp", None),
        P("expert", None, "dp"),
    )
    return jax.shard_map(
        local,
        mesh=mesh,
        in_specs=placed,
        out_specs=(
            P("expert", "dp"),
            P("expert", "dp", None),
            P("expert", "dp", None),
            P("expert", None, "dp"),
        ),
        check_vma=False,
    )
```

```python
import functools

import jax
import jax.numpy as jnp
from jax import lax
from jax.experimental import pallas as pl
from jax.experimental.pallas import tpu as pltpu
from jax.sharding import PartitionSpec as P

bf16 = jnp.bfloat16
f32 = jnp.float32
NX = 4
NZ = 2
BLK = 384


def call(body, ins, outs, scratch=(), steps=1, n_smem=0, hbm=(), out_hbm=True):
    def whole(shape):
        return pl.BlockSpec(shape, lambda i, n=len(shape): (0,) * n)

    def rowwise(shape, axis):
        block = tuple(v // steps if k == axis else v for k, v in enumerate(shape))
        return pl.BlockSpec(block, lambda i, n=len(shape), axis=axis: tuple(i if k == axis else 0 for k in range(n)))

    def run(*args):
        specs = [pl.BlockSpec(memory_space=pltpu.SMEM)] * n_smem
        args = list(args)
        for k in hbm:
            args[n_smem + k] = pltpu.with_memory_space_constraint(args[n_smem + k], pltpu.HBM)
        for v, axis in zip(args[n_smem:], ins, strict=True):
            specs.append(whole(v.shape) if axis is None else rowwise(v.shape, axis))
        return pl.pallas_call(
            body,
            grid=(steps,),
            out_shape=tuple((pltpu.HBM if hbm and out_hbm else jax.ShapeDtypeStruct)(s, d) for s, d, _ in outs),
            in_specs=specs,
            out_specs=tuple(whole(s) if axis is None else rowwise(s, axis) for s, _, axis in outs),
            scratch_shapes=list(scratch),
            compiler_params=pltpu.CompilerParams(vmem_limit_bytes=24 * 1024 * 1024),
        )(*args)

    return run


def dot(a, b, ca, cb):
    return lax.dot_general(a, b, (((ca,), (cb,)), ((), ())), preferred_element_type=f32)


def prep_body(routes_ref, weights_ref, tokens_ref, x_ref, sel_ref, w_ref, sel_s, *, experts, cap):
    top, tok = routes_ref.shape
    e_id = lax.broadcasted_iota(jnp.int32, (experts, tok), 0)
    names = jnp.zeros((experts, tok), f32)
    scale = jnp.zeros((experts, tok), f32)
    for k in range(top):
        hit = routes_ref[k : k + 1, :] == e_id
        names = jnp.where(hit, 1.0, names)
        scale = jnp.where(hit, weights_ref[k : k + 1, :], scale)
    row = lax.broadcasted_iota(jnp.int32, (tok, tok), 0)
    col = lax.broadcasted_iota(jnp.int32, (tok, tok), 1)
    earlier = jnp.where(row < col, 1.0, 0.0).astype(bf16)
    rank = dot(names.astype(bf16), earlier, 1, 0)
    rank = jnp.where(names > 0.0, rank, -1.0)
    slot = lax.broadcasted_iota(jnp.int32, (cap, tok), 0).astype(f32)
    for e in range(experts):
        here = rank[e : e + 1, :] == slot
        sel_s[e * cap : (e + 1) * cap, :] = jnp.where(here, 1.0, 0.0)
        w_ref[e * cap : (e + 1) * cap, :] = jnp.sum(
            jnp.where(here, scale[e : e + 1, :], 0.0), axis=1, keepdims=True
        )
    sel = sel_s[...].astype(bf16)
    sel_ref[...] = sel
    x_ref[...] = dot(sel, tokens_ref[...], 1, 0).astype(bf16)


def scale_body(sel_ref, w_ref, cot_ref, s_ref):
    s_ref[...] = (dot(sel_ref[...], cot_ref[...], 1, 0) * w_ref[...]).astype(bf16)


def lanes(tab, j):
    return pl.ds(pl.multiple_of(tab[j] * 128, 128), 128)


def beside(a, b):
    return jnp.concatenate([a, b], axis=1)


def gate_up_body(tab, x_ref, wg_ref, wu_ref, *outs):
    for t in range(NZ):
        for s, o in enumerate(outs):
            c = lanes(tab, t * NX + s)
            o[t] = dot(x_ref[...], beside(wg_ref[:, c], wu_ref[:, c]), 1, 0).astype(bf16)


def dhid_body(tab, s_ref, wd_ref, *refs):
    by_s, by_t, d_s = refs[:NX], refs[NX : NX + NZ], refs[-1]
    d_s[...] = dot(s_ref[...], wd_ref[...], 1, 1).astype(bf16)

    @pl.when(pl.program_id(0) == 0)
    def _():
        for t in range(NZ):
            for s in range(NX):
                by_s[s][t] = d_s[:, lanes(tab, t * NX + s)]

    @pl.when(pl.program_id(0) == 1)
    def _():
        for t in range(NZ):
            for s in range(NX):
                by_t[t][s] = d_s[:, lanes(tab, t * NX + s)]


def back_body(tab, *refs):
    gates, ups = refs[: NZ * NX], refs[NZ * NX : 2 * NZ * NX]
    wg_ref, wu_ref, back_ref, pg_ref, pu_ref = refs[-5:]
    total = None
    for q in range(NZ * NX):
        c = lanes(tab, q)
        g, u = gates[q][...], ups[q][...]
        pg_ref[:, c] = g
        pu_ref[:, c] = u
        t = dot(beside(g, u), beside(wg_ref[:, c], wu_ref[:, c]), 1, 1)
        total = t if total is None else total + t
    back_ref[...] = total.astype(bf16)


def hid_body(tab, *refs):
    own, left, right, far_0, far_1, o_ref = refs
    for z in range(NZ):
        for q, p in enumerate((own, left, right)):
            o_ref[:, lanes(tab, 4 * z + q)] = p[z]
    o_ref[:, lanes(tab, 3)] = far_0[...]
    o_ref[:, lanes(tab, 4 + 3)] = far_1[...]


def combine_body(sel_ref, ret_ref, o_ref):
    o_ref[...] = dot(sel_ref[...], ret_ref[...], 0, 0).astype(bf16)


def dp_perm(dz, dx):
    return [
        (z * NX + x, ((z + dz) % NZ) * NX + (x + dx) % NX) for z in range(NZ) for x in range(NX)
    ]


def move(v, dz, dx):
    return lax.ppermute(v, "dp", dp_perm(dz, dx))


def add(*parts):
    return sum(p.astype(f32) for p in parts)


def send_x(by_s):
    return [by_s[0]] + [move(by_s[s], 0, s) for s in range(1, NX)]


def sum_x_first(parts):
    other = move(add(*(p[1] for p in parts)).astype(bf16), 1, 0)
    return add(other, *(p[0] for p in parts))


def sum_z_first(by_t):
    other = move(by_t[1], 1, 0)
    sums = [add(by_t[0][s], other[s]) for s in range(NX)]
    return add(sums[0], *(move(sums[s].astype(bf16), 0, s) for s in range(1, NX)))


def gather(gate, up):
    gl, gr = move(gate, 0, 1), move(gate, 0, NX - 1)
    uz = move(up, 1, 0)
    ul, ur = move(up, 0, 1), move(up, 0, NX - 1)
    gates = [gate, gl, gr, move(gl, 0, 1)]
    gates += [move(v, 1, 0) for v in gates]
    uzl, uzr = move(uz, 0, 1), move(uz, 0, NX - 1)
    ups = [up, ul, ur, move(ur, 0, NX - 1), uz, uzl, uzr, move(uzl, 0, 1)]
    return gates + ups


def local(tokens, cotangent, routes, combine_weights, gate_weight, up_weight, down_weight):
    experts = lax.axis_size("expert")
    tok, top = routes.shape
    width = tokens.shape[1]
    hid = gate_weight.shape[2]
    cap = 3 * tok * top // (2 * experts)
    rows = experts * cap
    steps = rows // BLK
    wg, wu, wd = gate_weight[0], up_weight[0], down_weight[0]
    d = lax.axis_index("dp")
    z, x = d // NX, d % NX

    def table(shifts):
        s = jnp.array(shifts, jnp.int32)
        return (((z + jnp.arange(NZ))[:, None] % NZ) * NX + (x + s)[None, :] % NX).reshape(-1)

    dest = table((0, 1, 2, 3))
    orig = table((0, NX - 1, 1, 2))

    slots_x, sel, w_slot = call(
        functools.partial(prep_body, experts=experts, cap=cap),
        [None] * 3,
        [((rows, width), bf16, None), ((rows, tok), bf16, None), ((rows, 1), f32, None)],
        scratch=[pltpu.VMEM((rows, tok), f32)],
        hbm=(0, 1, 2),
        out_hbm=False,
    )(routes.T, combine_weights.T, tokens)
    (send_s,) = call(scale_body, [0, 0, None], [((rows, width), bf16, 0)], steps=steps)(
        sel, w_slot, cotangent
    )

    def a2a(v):
        return lax.all_to_all(
            v.reshape(experts, cap, width), "expert", split_axis=0, concat_axis=0, tiled=True
        ).reshape(rows, width)

    rows_x = a2a(slots_x)
    rows_x, send_s = lax.optimization_barrier((rows_x, send_s))
    gu = call(
        gate_up_body,
        [0, None, None],
        [((NZ, rows, 256), bf16, 1)] * NX,
        steps=steps,
        hbm=(0, 2),
        n_smem=1,
    )(dest, rows_x, wg, wu)
    gu = send_x(gu)
    rows_s = a2a(send_s)
    half = rows // 2
    dh = call(
        dhid_body,
        [0, None],
        [((NZ, half, 128), bf16, None)] * NX + [((NX, half, 128), bf16, None)] * NZ,
        scratch=[pltpu.VMEM((half, hid), bf16)],
        steps=2,
        hbm=(0, 1),
        n_smem=1,
    )(dest, rows_s, wd)
    gu, _ = lax.optimization_barrier((gu, dh[0]))
    gu = sum_x_first(gu)
    gate, upper = gu[:, :128], gu[:, 128:]
    sig = jax.nn.sigmoid(gate)
    act = gate * sig
    hidden = (act * upper).astype(bf16)
    slope = upper * (sig * (1.0 + gate * (1.0 - sig)))
    dh = jnp.concatenate([sum_x_first(send_x(dh[:NX])), sum_z_first(dh[NX:])], axis=0)
    back, pre_gate, pre_up = call(
        back_body,
        [0] * (2 * NZ * NX) + [None, None],
        [((rows, width), bf16, 0), ((rows, hid), bf16, 0), ((rows, hid), bf16, 0)],
        steps=steps,
        hbm=tuple(range(2 * NZ * NX)) + (2 * NZ * NX + 1,),
        n_smem=1,
    )(orig, *gather((dh * slope).astype(bf16), (dh * act).astype(bf16)), wg, wu)
    hidden_z = move(hidden, 1, 0)
    back, hidden, hidden_z = lax.optimization_barrier((back, hidden, hidden_z))
    returned = a2a(back)
    both = jnp.stack([hidden, hidden_z])
    left, right = move(both, 0, 1), move(both, 0, NX - 1)
    (hidden_all,) = call(
        hid_body, [1, 1, 1, 0, 0], [((rows, hid), bf16, 0)], steps=steps, n_smem=1, hbm=tuple(range(5))
    )(orig, both, left, right, move(left[0], 0, 1), move(right[1], 0, NX - 1))
    grad_gate = dot(rows_x, pre_gate, 0, 0).astype(bf16)[None]
    grad_up = dot(rows_x, pre_up, 0, 0).astype(bf16)[None]
    grad_down = dot(hidden_all, rows_s, 0, 0).astype(bf16)[None]
    (grad_tokens,) = call(combine_body, [None, None], [((tok, width), bf16, None)], hbm=(0,))(sel, returned)
    return (grad_tokens, grad_gate, grad_up, grad_down)


def solution(mesh):
    placed = (
        P("expert", "dp"),
        P("expert", "dp"),
        P("expert", None),
        P("expert", None),
        P("expert", "dp", None),
        P("expert", "dp", None),
        P("expert", None, "dp"),
    )
    return jax.shard_map(
        local,
        mesh=mesh,
        in_specs=placed,
        out_specs=(
            P("expert", "dp"),
            P("expert", "dp", None),
            P("expert", "dp", None),
            P("expert", None, "dp"),
        ),
        check_vma=False,
    )
```

```python
import functools

import jax
import jax.numpy as jnp
from jax import lax
from jax.experimental import pallas as pl
from jax.experimental.pallas import tpu as pltpu
from jax.sharding import PartitionSpec as P

bf16 = jnp.bfloat16
f32 = jnp.float32
NX = 4
NZ = 2
BLK = 384


def call(body, ins, outs, scratch=(), steps=1, n_smem=0, hbm=(), out_hbm=True):
    def whole(shape):
        return pl.BlockSpec(shape, lambda i, n=len(shape): (0,) * n)

    def rowwise(shape, axis):
        block = tuple(v // steps if k == axis else v for k, v in enumerate(shape))
        return pl.BlockSpec(block, lambda i, n=len(shape), axis=axis: tuple(i if k == axis else 0 for k in range(n)))

    def run(*args):
        specs = [pl.BlockSpec(memory_space=pltpu.SMEM)] * n_smem
        args = list(args)
        for k in hbm:
            args[n_smem + k] = pltpu.with_memory_space_constraint(args[n_smem + k], pltpu.HBM)
        for v, axis in zip(args[n_smem:], ins, strict=True):
            specs.append(whole(v.shape) if axis is None else rowwise(v.shape, axis))
        return pl.pallas_call(
            body,
            grid=(steps,),
            out_shape=tuple((pltpu.HBM if hbm and out_hbm else jax.ShapeDtypeStruct)(s, d) for s, d, _ in outs),
            in_specs=specs,
            out_specs=tuple(whole(s) if axis is None else rowwise(s, axis) for s, _, axis in outs),
            scratch_shapes=list(scratch),
            compiler_params=pltpu.CompilerParams(vmem_limit_bytes=24 * 1024 * 1024),
        )(*args)

    return run


def dot(a, b, ca, cb):
    return lax.dot_general(a, b, (((ca,), (cb,)), ((), ())), preferred_element_type=f32)


def prep_body(routes_ref, weights_ref, tokens_ref, x_ref, sel_ref, w_ref, sel_s, *, experts, cap):
    top, tok = routes_ref.shape
    e_id = lax.broadcasted_iota(jnp.int32, (experts, tok), 0)
    names = jnp.zeros((experts, tok), f32)
    scale = jnp.zeros((experts, tok), f32)
    for k in range(top):
        hit = routes_ref[k : k + 1, :] == e_id
        names = jnp.where(hit, 1.0, names)
        scale = jnp.where(hit, weights_ref[k : k + 1, :], scale)
    row = lax.broadcasted_iota(jnp.int32, (tok, tok), 0)
    col = lax.broadcasted_iota(jnp.int32, (tok, tok), 1)
    earlier = jnp.where(row < col, 1.0, 0.0).astype(bf16)
    rank = dot(names.astype(bf16), earlier, 1, 0)
    rank = jnp.where(names > 0.0, rank, -1.0)
    slot = lax.broadcasted_iota(jnp.int32, (cap, tok), 0).astype(f32)
    for e in range(experts):
        here = rank[e : e + 1, :] == slot
        sel_s[e * cap : (e + 1) * cap, :] = jnp.where(here, 1.0, 0.0)
        w_ref[e * cap : (e + 1) * cap, :] = jnp.sum(
            jnp.where(here, scale[e : e + 1, :], 0.0), axis=1, keepdims=True
        )
    sel = sel_s[...].astype(bf16)
    sel_ref[...] = sel
    x_ref[...] = dot(sel, tokens_ref[...], 1, 0).astype(bf16)


def scale_body(sel_ref, w_ref, cot_ref, s_ref):
    s_ref[...] = (dot(sel_ref[...], cot_ref[...], 1, 0) * w_ref[...]).astype(bf16)


def lanes(tab, j):
    return pl.ds(pl.multiple_of(tab[j] * 128, 128), 128)


def beside(a, b):
    return jnp.concatenate([a, b], axis=1)


def gate_up_body(tab, x_ref, wg_ref, wu_ref, *outs):
    for t in range(NZ):
        for s, o in enumerate(outs):
            c = lanes(tab, t * NX + s)
            o[t] = dot(x_ref[...], beside(wg_ref[:, c], wu_ref[:, c]), 1, 0).astype(bf16)


def dhid_body(tab, s_ref, wd_ref, *refs):
    by_s, by_t, d_s = refs[:NX], refs[NX : NX + NZ], refs[-1]
    d_s[...] = dot(s_ref[...], wd_ref[...], 1, 1).astype(bf16)

    @pl.when(pl.program_id(0) == 0)
    def _():
        for t in range(NZ):
            for s in range(NX):
                by_s[s][t] = d_s[:, lanes(tab, t * NX + s)]

    @pl.when(pl.program_id(0) == 1)
    def _():
        for t in range(NZ):
            for s in range(NX):
                by_t[t][s] = d_s[:, lanes(tab, t * NX + s)]


def back_body(tab, *refs):
    gates, ups = refs[: NZ * NX], refs[NZ * NX : 2 * NZ * NX]
    wg_ref, wu_ref, back_ref, pg_ref, pu_ref = refs[-5:]
    total = None
    for q in range(NZ * NX):
        c = lanes(tab, q)
        g, u = gates[q][...], ups[q][...]
        pg_ref[:, c] = g
        pu_ref[:, c] = u
        t = dot(beside(g, u), beside(wg_ref[:, c], wu_ref[:, c]), 1, 1)
        total = t if total is None else total + t
    back_ref[...] = total.astype(bf16)


def hid_body(tab, *refs):
    own, left, right, far_0, far_1, o_ref = refs
    for z in range(NZ):
        for q, p in enumerate((own, left, right)):
            o_ref[:, lanes(tab, 4 * z + q)] = p[z]
    o_ref[:, lanes(tab, 3)] = far_0[...]
    o_ref[:, lanes(tab, 4 + 3)] = far_1[...]


def combine_body(sel_ref, ret_ref, o_ref):
    o_ref[...] = dot(sel_ref[...], ret_ref[...], 0, 0).astype(bf16)


def dp_perm(dz, dx):
    return [
        (z * NX + x, ((z + dz) % NZ) * NX + (x + dx) % NX) for z in range(NZ) for x in range(NX)
    ]


def move(v, dz, dx):
    return lax.ppermute(v, "dp", dp_perm(dz, dx))


def add(*parts):
    return sum(p.astype(f32) for p in parts)


def send_x(by_s):
    return [by_s[0]] + [move(by_s[s], 0, s) for s in range(1, NX)]


def other_z(parts):
    return add(*(p[1] for p in parts)).astype(bf16)


def sum_x_first(parts):
    return add(move(other_z(parts), 1, 0), *(p[0] for p in parts))


def sum_z_first(by_t):
    other = move(by_t[1], 1, 0)
    sums = [add(by_t[0][s], other[s]) for s in range(NX)]
    return add(sums[0], *(move(sums[s].astype(bf16), 0, s) for s in range(1, NX)))


def gather(gate, up):
    gl, gr = move(gate, 0, 1), move(gate, 0, NX - 1)
    uz = move(up, 1, 0)
    ul, ur = move(up, 0, 1), move(up, 0, NX - 1)
    gates = [gate, gl, gr, move(gl, 0, 1)]
    gates += [move(v, 1, 0) for v in gates]
    uzl, uzr = move(uz, 0, 1), move(uz, 0, NX - 1)
    ups = [up, ul, ur, move(ur, 0, NX - 1), uz, uzl, uzr, move(uzl, 0, 1)]
    return gates + ups


def local(tokens, cotangent, routes, combine_weights, gate_weight, up_weight, down_weight):
    experts = lax.axis_size("expert")
    tok, top = routes.shape
    width = tokens.shape[1]
    hid = gate_weight.shape[2]
    cap = 3 * tok * top // (2 * experts)
    rows = experts * cap
    steps = rows // BLK
    wg, wu, wd = gate_weight[0], up_weight[0], down_weight[0]
    d = lax.axis_index("dp")
    z, x = d // NX, d % NX

    def table(shifts):
        s = jnp.array(shifts, jnp.int32)
        return (((z + jnp.arange(NZ))[:, None] % NZ) * NX + (x + s)[None, :] % NX).reshape(-1)

    dest = table((0, 1, 2, 3))
    orig = table((0, NX - 1, 1, 2))

    slots_x, sel, w_slot = call(
        functools.partial(prep_body, experts=experts, cap=cap),
        [None] * 3,
        [((rows, width), bf16, None), ((rows, tok), bf16, None), ((rows, 1), f32, None)],
        scratch=[pltpu.VMEM((rows, tok), f32)],
        hbm=(0, 1, 2),
        out_hbm=False,
    )(routes.T, combine_weights.T, tokens)
    (send_s,) = call(scale_body, [0, 0, None], [((rows, width), bf16, 0)], steps=steps)(
        sel, w_slot, cotangent
    )

    def a2a(v):
        return lax.all_to_all(
            v.reshape(experts, cap, width), "expert", split_axis=0, concat_axis=0, tiled=True
        ).reshape(rows, width)

    rows_x = a2a(slots_x)
    rows_x, send_s = lax.optimization_barrier((rows_x, send_s))
    gu = call(
        gate_up_body,
        [0, None, None],
        [((NZ, rows, 256), bf16, 1)] * NX,
        steps=steps,
        hbm=(0, 2),
        n_smem=1,
    )(dest, rows_x, wg, wu)
    gu = send_x(gu)
    rows_s = a2a(send_s)
    half = rows // 2
    dh = call(
        dhid_body,
        [0, None],
        [((NZ, half, 128), bf16, None)] * NX + [((NX, half, 128), bf16, None)] * NZ,
        scratch=[pltpu.VMEM((half, hid), bf16)],
        steps=2,
        hbm=(0, 1),
        n_smem=1,
    )(dest, rows_s, wd)
    gu, _ = lax.optimization_barrier((gu, dh[0]))
    dh_x, gu_z = send_x(dh[:NX]), other_z(gu)
    dh_x, _ = lax.optimization_barrier((dh_x, gu_z))
    gu = add(move(gu_z, 1, 0), *(p[0] for p in gu))
    gate, upper = gu[:, :128], gu[:, 128:]
    sig = jax.nn.sigmoid(gate)
    act = gate * sig
    hidden = (act * upper).astype(bf16)
    slope = upper * (sig * (1.0 + gate * (1.0 - sig)))
    dh = jnp.concatenate([sum_x_first(dh_x), sum_z_first(dh[NX:])], axis=0)
    back, pre_gate, pre_up = call(
        back_body,
        [0] * (2 * NZ * NX) + [None, None],
        [((rows, width), bf16, 0), ((rows, hid), bf16, 0), ((rows, hid), bf16, 0)],
        steps=steps,
        hbm=tuple(range(2 * NZ * NX)) + (2 * NZ * NX + 1,),
        n_smem=1,
    )(orig, *gather((dh * slope).astype(bf16), (dh * act).astype(bf16)), wg, wu)
    hidden_z = move(hidden, 1, 0)
    back, hidden, hidden_z = lax.optimization_barrier((back, hidden, hidden_z))
    returned = a2a(back)
    both = jnp.stack([hidden, hidden_z])
    left, right = move(both, 0, 1), move(both, 0, NX - 1)
    (hidden_all,) = call(
        hid_body, [1, 1, 1, 0, 0], [((rows, hid), bf16, 0)], steps=steps, n_smem=1, hbm=tuple(range(5))
    )(orig, both, left, right, move(left[0], 0, 1), move(right[1], 0, NX - 1))
    grad_gate = dot(rows_x, pre_gate, 0, 0).astype(bf16)[None]
    grad_up = dot(rows_x, pre_up, 0, 0).astype(bf16)[None]
    grad_down = dot(hidden_all, rows_s, 0, 0).astype(bf16)[None]
    (grad_tokens,) = call(combine_body, [None, None], [((tok, width), bf16, None)], hbm=(0,))(sel, returned)
    return (grad_tokens, grad_gate, grad_up, grad_down)


def solution(mesh):
    placed = (
        P("expert", "dp"),
        P("expert", "dp"),
        P("expert", None),
        P("expert", None),
        P("expert", "dp", None),
        P("expert", "dp", None),
        P("expert", None, "dp"),
    )
    return jax.shard_map(
        local,
        mesh=mesh,
        in_specs=placed,
        out_specs=(
            P("expert", "dp"),
            P("expert", "dp", None),
            P("expert", "dp", None),
            P("expert", None, "dp"),
        ),
        check_vma=False,
    )
```
